32 devices in a mesh: dp: 4 (over y, x), mp: 8 (over z, core).
Axes of the slice: x: 2, y: 2, z: 4, core: 2. Of those that a mesh axis runs over, the one named last changes fastest.
Arguments:
- x_in: bfloat16 [2048, 4096], P('dp', 'mp'), may hold values from -6 to 6
- hidden_act: bfloat16 [2048, 14336], P('dp', 'mp'), may hold values from -6 to 6
- w_down: bfloat16 [14336, 4096], P('mp'), may hold values from -0.0625 to 0.0625
- y_cot: bfloat16 [2048, 4096], P('dp', 'mp'), may hold values from -5 to 5
- picked: int32 [4, 32], replicated, may hold values from 0 to 511, as said below
- owner: int32 [4, 32, 1], replicated, may hold values from 0 to 3; in each aligned block of 32 rows (0 to 31, 32 to 63, ..., all dimensions but the last counted through in order) at most 8 rows name the same one
- w_proj: bfloat16 [4096, 2048], P('mp'), may hold values from -0.09375 to 0.09375
- pos_embed: bfloat16 [32, 2048], replicated, may hold values from -6 to 6
- norm_gain: bfloat16 [2048], replicated, may hold values from 0.25 to 1.75
- w_gate_dec: bfloat16 [2048, 8192], P(None, 'mp'), may hold values from -0.125 to 0.125
- w_up_dec: bfloat16 [2048, 8192], P(None, 'mp'), may hold values from -0.125 to 0.125
Outputs:
- y_out: bfloat16 [2048, 4096], P('dp', 'mp')
- grad_hidden: bfloat16 [2048, 14336], P('dp', 'mp')
- grad_down: float32 [14336, 4096], P('mp', 'dp')
- dec_hidden: bfloat16 [4096, 8192], P('dp', 'mp')
The draws below stay inside these ranges and needn't reach their ends.
Inputs may be any that keep to these rules, and one draw needn't show every extreme that they name: `picked`: each row lists 32 frame positions in increasing order, one in each aligned block of 16 frames; the first and the last frame of every window are listed. In each window at most 8 selected frames have the same owner, and in some window one owner (4 * 8) has exactly 8.
All inputs are finite; a program needn't handle non-finite values.
Results may differ from the reference program's by a relative error of at most 0.025.
Values may be sent and summed in bfloat16 or wider, within the bound.
No kernel may reach another device: no remote copies, remote signals or barrier semaphores. Data moves between devices by JAX's collectives and lax.ppermute only.
A program may use at most 192 MiB of HBM per device.

```python
import math
import jax
import jax.numpy as jnp
import numpy as np
from jax import lax

D = 4096
FF = 14336
DW = 2048
DFF = 8192
CB = 32
FRAMES = 512
WINDOWS = 4
TOKENS = 2048
NSEL = 32
CAP = 8
SLOTS = 32


def draw_picked(key, part):
    offsets = jax.random.randint(key, (WINDOWS, NSEL), 0, 16)
    column = jnp.arange(NSEL, dtype=jnp.int32)
    offsets = jnp.where(column[None, :] == 0, 0, offsets)
    offsets = jnp.where(column[None, :] == NSEL - 1, 15, offsets)
    return (16 * column[None, :] + offsets).astype(jnp.int32)


def strengthened(entries, own_key, source, target, blocks, factor):
    def block_of(axis_at):
        return (jnp.arange(entries.shape[axis_at]) // (entries.shape[axis_at] // blocks)).reshape((-1,) + (1,) * (entries.ndim - 1 - axis_at))

    first = jax.random.permutation(own_key, blocks)[block_of(target)]
    other_side = (block_of(target) + blocks // 2) % blocks
    return jnp.where((block_of(source) == first) | (block_of(source) == other_side), factor * entries, entries)


def levels(own_key, extent, cuts, least, high):
    level, own = 1.0, jax.random.fold_in(own_key, 6)
    for dim, blocks in cuts:
        heights = jnp.exp(jax.random.uniform(jax.random.fold_in(own, dim), (blocks,), jnp.float32, least / len(cuts), high / len(cuts)))
        level = level * jnp.repeat(heights, extent[dim] // blocks).reshape([-1 if axis == dim else 1 for axis in range(len(extent))])
    return level


def deal_out(rng, own, number, rows, count, top, reach, slope):
    sequence = jax.random.permutation(rng, count)
    crowded, common = shares(count, rows * top, reach, slope, True), shares(count, rows * top, reach, slope, False)
    places = jnp.arange(count)

    def named(lengths, turn):
        used = int((lengths > 0).sum())
        fixed = max(1, used // 4)
        shifted = fixed + (places - fixed + turn * (used - fixed)) % max(1, count - fixed)
        return jnp.zeros((count,), jnp.int32).at[sequence[jnp.where(places < fixed, places, shifted)]].set(jnp.asarray(lengths, jnp.int32))

    lengths = jnp.where(number % 4 == 0, named(crowded, number // 4), named(common, number - number // 4 - 1))
    mixed = jax.random.permutation(jax.random.fold_in(own, 3), count)
    giver, sink = mixed[0:count // 2 * 2:2], mixed[1:count // 2 * 2:2]
    slack = jnp.minimum(lengths[giver] - 1, reach - lengths[sink]) // 2
    slack = jnp.where((giver == sequence[0]) | (sink == sequence[0]) | (lengths[sink] == 0), 0, jnp.maximum(slack, 0))
    shifted = jax.random.randint(jax.random.fold_in(own, 4), (count // 2,), 0, 1 << 20) % (slack + 1)
    lengths = lengths.at[giver].add(-shifted).at[sink].add(shifted)
    members = jnp.searchsorted(jnp.cumsum(lengths), jnp.arange(rows * top), side="right").astype(jnp.int32)
    grid = members.reshape(top, rows).T
    grid = grid[jax.random.permutation(jax.random.fold_in(own, 1), rows)]
    turn = jax.random.randint(jax.random.fold_in(own, 2), (rows, 1), 0, top)
    return jnp.take_along_axis(grid, (jnp.arange(top)[None, :] + turn) % top, axis=1)


def shares(number_of, total, bound, lean, full):
    loads = [(1 << 20) // math.isqrt(rank ** lean) + 1 for rank in range(1, number_of + 1)]
    largest = bound if full else min(bound, max(-(-total // number_of), total * loads[0] // sum(loads)))
    least = 1 if total - largest >= number_of - 1 else 0
    counts, surplus = [largest] + [least] * (number_of - 1), total - largest - least * (number_of - 1)
    while surplus > 0:
        movable = [i for i in range(1, number_of) if counts[i] < largest] or [i for i in range(1, number_of) if counts[i] < bound]
        whole, left = sum([loads[i] for i in movable]), surplus
        for i in movable:
            more = min(bound - counts[i], max(1, left * loads[i] // whole), surplus)
            counts[i] = counts[i] + more
            surplus = surplus - more
    return np.array(counts)


def noise(rng, extent, scale, limit, pieces=(), kind=jnp.bfloat16):
    drawn = jax.random.normal(rng, extent, jnp.float32) * scale
    if len(pieces) > 0:
        drawn = levels(rng, extent, pieces, -0.22, 0.18) * drawn
    return jnp.clip(drawn, min=-limit, max=limit).astype(kind)


def bell_draw_with(rng, dims, scale, reach, pieces, heavy, kind=jnp.bfloat16):
    values = scale * jax.random.normal(rng, dims, jnp.float32)
    if pieces:
        values = values * levels(rng, dims, pieces, -0.22, 0.18)
    return jnp.clip(strengthened(values, jax.random.fold_in(rng, 3), *heavy), -reach, reach).astype(kind)


def setup_inputs(seed: int = 0) -> dict:
    streams_of = jax.random.split(jax.random.key(seed), 12)
    x_in = noise(streams_of[0], (TOKENS, D), 1.0, 6.0, ((0, 4), (1, 8)))
    hidden_act = noise(streams_of[1], (TOKENS, FF), 1.0, 6.0, ((0, 4), (1, 8)))
    w_down = bell_draw_with(streams_of[2], (FF, D), FF ** -0.5, 0.0625, ((0, 8),), (0, 1, 8, 2.0))
    y_cot = bell_draw_with(streams_of[3], (TOKENS, D), 0.25, 5.0, ((0, 4), (1, 8)), (0, 1, 8, 2.0))
    picked = draw_picked(jax.random.fold_in(streams_of[11], 71), 0)
    owner_keys = jax.random.split(jax.random.fold_in(streams_of[5], 1), WINDOWS * NSEL // NSEL)
    owner_turns = jax.random.permutation(jax.random.fold_in(streams_of[5], 3), WINDOWS * NSEL // NSEL)
    owner = jax.vmap(lambda own, number: deal_out(jax.random.fold_in(streams_of[5], 2), own, number, NSEL, WINDOWS, 1, CAP, 2))(owner_keys, owner_turns).reshape((WINDOWS, NSEL, 1))
    w_proj = noise(streams_of[6], (D, DW), D ** -0.5, 0.09375, ((0, 8),))
    pos_embed = noise(streams_of[7], (CB, DW), 1.0, 6.0)
    norm_gain = jnp.clip(1.0 + 0.15 * jax.random.normal(streams_of[8], (DW,), jnp.float32), 0.25, 1.75).astype(jnp.bfloat16)
    w_gate_dec = noise(streams_of[9], (DW, DFF), DW ** -0.5, 0.125, ((1, 8),))
    w_up_dec = noise(streams_of[10], (DW, DFF), DW ** -0.5, 0.125, ((1, 8),))
    return dict(x_in=x_in, hidden_act=hidden_act, w_down=w_down, y_cot=y_cot, picked=picked, owner=owner, w_proj=w_proj, pos_embed=pos_embed, norm_gain=norm_gain, w_gate_dec=w_gate_dec, w_up_dec=w_up_dec)


eps_norm = 1e-05

def slot_ranks(owners):
    length = owners.shape[-1]
    position = jnp.arange(length, dtype=jnp.int32)
    earlier = position[:, None] > position[None, :]
    same_owner = owners[..., :, None] == owners[..., None, :]
    return lax.optimization_barrier(jnp.sum((earlier & same_owner).astype(jnp.int32), axis=-1))

def decoder_rows(z_rows, occupied_rows, pos_embed, norm_gain, w_gate_dec, w_up_dec):
    dec_input = z_rows[:, None, :] + pos_embed.astype(jnp.float32)[None, :, :]
    inverse_rms = lax.rsqrt(lax.optimization_barrier(jnp.mean(dec_input * dec_input, axis=-1, keepdims=True)) + eps_norm)
    normed = (dec_input * inverse_rms * norm_gain.astype(jnp.float32)).astype(jnp.bfloat16)
    normed = normed.reshape(-1, normed.shape[-1])
    gate_out = jnp.dot(normed, w_gate_dec, preferred_element_type=jnp.float32)
    up_out = jnp.dot(normed, w_up_dec, preferred_element_type=jnp.float32)
    keep_rows = jnp.repeat(occupied_rows, pos_embed.shape[0])[:, None]
    return (jax.nn.silu(gate_out) * up_out * keep_rows).astype(jnp.bfloat16)

def reference(x_in, hidden_act, w_down, y_cot, picked, owner, w_proj, pos_embed, norm_gain, w_gate_dec, w_up_dec):
    summed = jnp.dot(hidden_act, w_down, preferred_element_type=jnp.float32)
    y_out = (x_in.astype(jnp.float32) + summed).astype(jnp.bfloat16)
    grad_hidden = lax.dot_general(y_cot, w_down, (((1,), (1,)), ((), ())), preferred_element_type=jnp.float32).astype(jnp.bfloat16)
    acts_all = hidden_act.reshape(WINDOWS, FRAMES, FF)
    cots_all = y_cot.reshape(WINDOWS, FRAMES, D)

    def add_window(running, window):
        window_part = lax.dot_general(window[0], window[1], (((0,), (0,)), ((), ())), preferred_element_type=jnp.float32)
        rounded = lax.optimization_barrier(window_part.astype(jnp.bfloat16))
        return (running + rounded.astype(jnp.float32), None)
    running, _ = lax.scan(add_window, jnp.zeros((FF, D), jnp.float32), (acts_all, cots_all))
    grad_down = running / WINDOWS
    owners = owner[:, :, 0]
    slot_rank = slot_ranks(owners)
    window_ids = jnp.arange(WINDOWS, dtype=jnp.int32)[:, None]
    dest_slot = ((owners * WINDOWS + window_ids) * CAP + slot_rank).reshape(-1).astype(jnp.int32)
    source_row = (window_ids * FRAMES + picked).reshape(-1).astype(jnp.int32)
    frames = jnp.zeros((WINDOWS * SLOTS, D), jnp.bfloat16).at[dest_slot].set(y_out[source_row])
    occupied = jnp.zeros((WINDOWS * SLOTS,), jnp.float32).at[dest_slot].set(1.0)
    z_all = jnp.dot(frames, w_proj, preferred_element_type=jnp.float32)

    def decode(inputs):
        return decoder_rows(inputs[0], inputs[1], pos_embed, norm_gain, w_gate_dec, w_up_dec)
    dec_hidden = lax.map(decode, (z_all.reshape(WINDOWS, SLOTS, DW), occupied.reshape(WINDOWS, SLOTS)))
    dec_hidden = dec_hidden.reshape(WINDOWS * SLOTS * CB, DFF)
    return (y_out, grad_hidden, grad_down, dec_hidden)
```

```python
import jax
import jax.numpy as jnp
from jax import lax
from jax.experimental import pallas as pl
from jax.experimental.pallas import tpu as pltpu
from jax.sharding import PartitionSpec as P

CAP = 8

eps_norm = 1e-05

F32 = jnp.float32
BF16 = jnp.bfloat16


def slot_ranks(owners):
    length = owners.shape[-1]
    position = jnp.arange(length, dtype=jnp.int32)
    earlier = position[:, None] > position[None, :]
    same_owner = owners[..., :, None] == owners[..., None, :]
    return jnp.sum((earlier & same_owner).astype(jnp.int32), axis=-1)


def frame_slots(picked, owners, window_index, groups):
    my_owners = lax.dynamic_index_in_dim(owners, window_index, 0, keepdims=False)
    my_picked = lax.dynamic_index_in_dim(picked, window_index, 0, keepdims=False)
    target = my_owners * CAP + slot_ranks(my_owners)
    slot_ids = jnp.arange(groups * CAP, dtype=jnp.int32)
    slot_match = (target[None, :] == slot_ids[:, None]).astype(jnp.int32)
    frame_rows = jnp.sum(slot_match * my_picked[None, :], axis=1)
    return frame_rows, jnp.sum(slot_match, axis=1)


def occupied_slots(owners, window_index):
    per_window = jnp.sum((owners == window_index).astype(jnp.int32), axis=1)
    return (
        (jnp.arange(CAP, dtype=jnp.int32)[None, :] < per_window[:, None])
        .astype(F32)
        .reshape(-1)
    )


def decoder_rows(z_rows, occupied_rows, pos_embed, norm_gain, w_gate_dec, w_up_dec):
    dec_input = z_rows[:, None, :] + pos_embed.astype(F32)[None, :, :]
    inverse_rms = lax.rsqrt(jnp.mean(dec_input * dec_input, axis=-1, keepdims=True) + eps_norm)
    normed = (dec_input * inverse_rms * norm_gain.astype(F32)).astype(BF16)
    normed = normed.reshape(-1, normed.shape[-1])
    gate_out = jnp.dot(normed, w_gate_dec, preferred_element_type=F32)
    up_out = jnp.dot(normed, w_up_dec, preferred_element_type=F32)
    keep_rows = jnp.repeat(occupied_rows, pos_embed.shape[0])[:, None]
    return (jax.nn.silu(gate_out) * up_out * keep_rows).astype(BF16)


def any_mesh(
    x_in, hidden_act, w_down, y_cot, picked, owner, w_proj, pos_embed, norm_gain, w_gate_dec, w_up_dec
):
    groups = lax.axis_size("dp")
    window_index = lax.axis_index("dp")
    partial_term = jnp.dot(hidden_act, w_down, preferred_element_type=F32)
    summed = lax.psum_scatter(
        partial_term.astype(BF16), "mp", scatter_dimension=1, tiled=True
    ).astype(F32)
    y_out = (x_in.astype(F32) + summed).astype(BF16)
    full_cot = lax.all_gather(y_cot, "mp", axis=1, tiled=True)
    grad_rows = lax.dot_general(
        full_cot, w_down, (((1,), (1,)), ((), ())), preferred_element_type=F32
    )
    grad_weight = lax.dot_general(
        hidden_act, full_cot, (((0,), (0,)), ((), ())), preferred_element_type=F32
    )
    grad_hidden = grad_rows.astype(BF16)
    window_part = grad_weight.astype(BF16)
    grad_down = (
        lax.psum_scatter(window_part, "dp", scatter_dimension=1, tiled=True).astype(F32) / groups
    )
    owners = owner[:, :, 0]
    frame_rows, filled = frame_slots(picked, owners, window_index, groups)
    outgoing = jnp.take(y_out, frame_rows, axis=0) * filled.astype(BF16)[:, None]
    feature_width = outgoing.shape[1]
    arrived = lax.all_to_all(
        outgoing.reshape(groups, CAP, feature_width), "dp", split_axis=0, concat_axis=0, tiled=True
    )
    arrived = arrived.reshape(groups * CAP, feature_width)
    occupied = occupied_slots(owners, window_index)
    z_part = jnp.dot(arrived, w_proj, preferred_element_type=F32)
    z_rows = lax.psum(z_part.astype(BF16), "mp").astype(F32)
    dec_hidden = decoder_rows(z_rows, occupied, pos_embed, norm_gain, w_gate_dec, w_up_dec)
    return (y_out, grad_hidden, grad_down, dec_hidden)


RESIDENT = pl.BlockSpec(memory_space=pltpu.VMEM)
SCALARS = pl.BlockSpec(memory_space=pltpu.SMEM)
IN_PLACE = pl.BlockSpec(memory_space=pl.ANY)


def nbytes(*arrays):
    return sum(a.size * a.dtype.itemsize for a in arrays)


def kernel_params(scratch_mib):
    return pltpu.CompilerParams(vmem_limit_bytes=scratch_mib * 1024 * 1024)


def block(index, size):
    return pl.ds(pl.multiple_of(index * size, size), size)


def down_blocks(core, hidden, w_down, select, bw):
    rows, ff = hidden.shape
    nblk = w_down.shape[1] // (2 * bw)
    slots = select.shape[0]

    def body(c_ref, h_ref, w_ref, s_ref, theirs_ref, mine_ref, sel_theirs_ref, sel_mine_ref):
        for parity, out_ref, sel_ref in (
            (1 - c_ref[0], theirs_ref, sel_theirs_ref),
            (c_ref[0], mine_ref, sel_mine_ref),
        ):
            for j in range(nblk):
                w = w_ref[:, block(2 * j + parity, bw)]
                part = jnp.dot(h_ref[...], w, preferred_element_type=F32).astype(BF16)
                out_ref[j] = part
                sel_ref[j] = jnp.dot(s_ref[...], part, preferred_element_type=F32).astype(BF16)

    big = jax.ShapeDtypeStruct((nblk, rows, bw), BF16)
    small = jax.ShapeDtypeStruct((nblk, slots, bw), BF16)
    return pl.pallas_call(
        body,
        out_shape=(big, big, small, small),
        in_specs=[SCALARS, RESIDENT, RESIDENT, RESIDENT],
        out_specs=(RESIDENT,) * 4,
        compiler_params=kernel_params(8),
        name="down_blocks",
        cost_estimate=pl.CostEstimate(
            flops=4 * rows * ff * nblk * bw,
            bytes_accessed=nbytes(hidden, w_down) + 8 * rows * nblk * bw,
            transcendentals=0,
        ),
    )(core, hidden, w_down, select)


def gather_cot(where, near, near_swapped, far, far_swapped):
    _, rows, bw = near.shape
    half = rows // 2
    sources = (near, near_swapped, far, far_swapped)

    def body(w_ref, n_ref, ns_ref, f_ref, fs_ref, full_ref, own_ref, p1_ref, p2_ref, p3_ref):
        for i, ref in enumerate((n_ref, ns_ref, f_ref, fs_ref)):
            for k in range(2):
                full_ref[:, block(w_ref[2 + 2 * i + k], bw)] = ref[k]
        d, c = w_ref[0], w_ref[1]
        own_ref[...] = full_ref[:, block(d, 2 * bw)]
        for flip, ref in ((1, p1_ref), (2, p2_ref), (3, p3_ref)):
            ref[...] = full_ref[block(c, half), block(d ^ flip, 2 * bw)]

    part = jax.ShapeDtypeStruct((half, 2 * bw), BF16)
    return pl.pallas_call(
        body,
        out_shape=(
            jax.ShapeDtypeStruct((rows, 8 * bw), BF16),
            jax.ShapeDtypeStruct((rows, 2 * bw), BF16),
            part,
            part,
            part,
        ),
        in_specs=[SCALARS] + [RESIDENT] * 4,
        out_specs=(RESIDENT,) * 5,
        compiler_params=kernel_params(2),
        name="gather_cot",
        cost_estimate=pl.CostEstimate(
            flops=0, bytes_accessed=3 * nbytes(*sources), transcendentals=0
        ),
    )(where, *sources)


def rows_grad(full_cot, w_down, tn=256):
    rows, dm = full_cot.shape
    ff = w_down.shape[0]

    def body(b_ref, w_ref, out_ref):
        for j in range(ff // tn):
            out_ref[:, j * tn : (j + 1) * tn] = lax.dot_general(
                b_ref[...],
                w_ref[j * tn : (j + 1) * tn, :],
                (((1,), (1,)), ((), ())),
                preferred_element_type=F32,
            ).astype(BF16)

    return pl.pallas_call(
        body,
        out_shape=jax.ShapeDtypeStruct((rows, ff), BF16),
        in_specs=[RESIDENT] * 2,
        out_specs=RESIDENT,
        compiler_params=kernel_params(8),
        name="rows_grad",
        cost_estimate=pl.CostEstimate(
            flops=2 * rows * ff * dm,
            bytes_accessed=nbytes(full_cot, w_down) + 2 * rows * ff,
            transcendentals=0,
        ),
    )(full_cot, w_down)


def weight_grad(core, pairs, scale, base=None, tm=256):
    ff = pairs[0][0].shape[1]
    cols = pairs[0][1].shape[1]
    hs, ys = [], []
    for h, y, _ in pairs:
        if not any(h is g for g in hs):
            hs.append(h)
        ys.append(y)
    where = [next(i for i, g in enumerate(hs) if g is h) for h, _, _ in pairs]
    nh, ny = len(hs), len(ys)
    tiles = ff // tm

    def body(c_ref, *refs):
        h_refs, y_refs = refs[:nh], refs[nh : nh + ny]

        def tile(j):
            acc = None
            for i, (_, _, half) in enumerate(pairs):
                h_ref, tokens = h_refs[where[i]], ys[i].shape[0]
                cut = slice(j * tm, (j + 1) * tm)
                if half is None:
                    h = h_ref[:, cut]
                else:
                    first = c_ref[0] if half == 0 else 1 - c_ref[0]
                    h = h_ref[block(first, tokens), cut]
                term = lax.dot_general(
                    h, y_refs[i][...], (((0,), (0,)), ((), ())), preferred_element_type=F32
                )
                acc = term if acc is None else acc + term
            return acc * scale

        if base is None:
            out_ref = refs[nh + ny]
            for j in range(tiles):
                out_ref[j * tm : (j + 1) * tm, :] = tile(j)
            return
        base_ref, out_ref, buf, sems = refs[nh + ny :]
        copies = []
        for j in range(tiles):
            if j >= 2:
                copies[j - 2].wait()
            buf[j % 2] = tile(j) + base_ref[j * tm : (j + 1) * tm, :]
            copies.append(
                pltpu.make_async_copy(
                    buf.at[j % 2], out_ref.at[pl.ds(j * tm, tm), :], sems.at[j % 2]
                )
            )
            copies[j].start()
        for copy in copies[-2:]:
            copy.wait()

    args = hs + ys + ([] if base is None else [base])
    return pl.pallas_call(
        body,
        out_shape=jax.ShapeDtypeStruct((ff, cols), F32),
        in_specs=[SCALARS] + [RESIDENT] * len(args),
        out_specs=RESIDENT if base is None else IN_PLACE,
        scratch_shapes=[]
        if base is None
        else [pltpu.VMEM((2, tm, cols), F32), pltpu.SemaphoreType.DMA((2,))],
        compiler_params=kernel_params(12),
        name="weight_grad",
        cost_estimate=pl.CostEstimate(
            flops=sum(2 * ff * y.size for y in ys),
            bytes_accessed=nbytes(*args) + 4 * ff * cols,
            transcendentals=0,
        ),
    )(core, *args)


def decoder(z, keep, pos, gain, w_gate, w_up, tn=256):
    slots, dw = z.shape
    cb = pos.shape[0]
    dff = w_gate.shape[1]

    def body(z_ref, keep_ref, pos_ref, g_ref, wg_ref, wu_ref, o_ref, n_ref):
        def one(r, carry):
            row = z_ref[pl.ds(r, 1), :] + pos_ref[...].astype(F32)
            inverse = lax.rsqrt(jnp.mean(row * row, axis=-1, keepdims=True) + eps_norm)
            n_ref[block(r, cb), :] = (row * inverse * g_ref[...].astype(F32)).astype(BF16)
            return carry

        lax.fori_loop(0, slots, one, 0, unroll=4)
        for j in range(dff // tn):
            cut = slice(j * tn, (j + 1) * tn)
            gate = jnp.dot(n_ref[...], wg_ref[:, cut], preferred_element_type=F32)
            up = jnp.dot(n_ref[...], wu_ref[:, cut], preferred_element_type=F32)
            o_ref[:, cut] = (gate / (1.0 + jnp.exp(-gate)) * up * keep_ref[...]).astype(BF16)

    return pl.pallas_call(
        body,
        out_shape=jax.ShapeDtypeStruct((slots * cb, dff), BF16),
        in_specs=[RESIDENT] * 6,
        out_specs=RESIDENT,
        scratch_shapes=[pltpu.VMEM((slots * cb, dw), BF16)],
        compiler_params=kernel_params(16),
        name="decoder",
        cost_estimate=pl.CostEstimate(
            flops=4 * slots * cb * dff * dw,
            bytes_accessed=2 * (2 * dw * dff + slots * cb * dff),
            transcendentals=slots * cb * dff,
        ),
    )(z, keep, pos, gain, w_gate, w_up)


def chips_move(x, moves):
    return lax.ppermute(x, "mp", [(2 * a + c, 2 * b + c) for a, b in moves for c in range(2)])


def cores_swap(x):
    return lax.ppermute(x, "mp", [(i, i ^ 1) for i in range(8)])


def windows_swap(x, flip):
    return lax.ppermute(x, "dp", [(i, i ^ flip) for i in range(4)])


PAIR = [(0, 1), (1, 0), (2, 3), (3, 2)]
MIDDLE = [(1, 2), (2, 1)]
OUTWARD = [(1, 0), (2, 3)]
INWARD = [(0, 1), (3, 2)]
FAR = [(0, 2), (1, 3), (2, 0), (3, 1)]


def at(blocks, index):
    return lax.dynamic_index_in_dim(blocks, index, 0, keepdims=False)


def add(*terms):
    return sum(t.astype(F32) for t in terms[1:]) + terms[0].astype(F32)


def small_slice(
    x_in, hidden_act, w_down, y_cot, picked, owner, w_proj, pos_embed, norm_gain, w_gate_dec, w_up_dec
):
    groups = 4
    d = lax.axis_index("dp")
    m = lax.axis_index("mp")
    z, c = m // 2, m % 2
    low = z < 2
    middle = (z == 1) | (z == 2)
    rows, bw = x_in.shape
    core = jnp.reshape(c, (1,)).astype(jnp.int32)

    h_x = windows_swap(hidden_act, 1)
    h_y = windows_swap(hidden_act, 2)
    half = rows // 2
    h_d0 = windows_swap(lax.dynamic_slice_in_dim(h_x, c * half, half, 0), 2)
    h_d1 = windows_swap(lax.dynamic_slice_in_dim(h_y, (1 - c) * half, half, 0), 1)

    r_pair = chips_move(y_cot, PAIR)
    r_mid0 = chips_move(y_cot, MIDDLE)
    r_mid1 = chips_move(r_pair, MIDDLE)
    r_out0 = chips_move(r_mid0, OUTWARD)
    r_out1 = chips_move(r_mid1, OUTWARD)
    near = jnp.stack([y_cot, r_pair])
    far = jnp.stack([jnp.where(middle, r_mid0, r_out0), jnp.where(middle, r_mid1, r_out1)])
    near_ids = jnp.stack([z, z ^ 1])
    far_ids = jnp.stack([jnp.where(low, 2, 1), jnp.where(low, 3, 0)])
    where = jnp.concatenate(
        [
            jnp.stack([d, c]),
            2 * near_ids + c,
            2 * near_ids + 1 - c,
            2 * far_ids + c,
            2 * far_ids + 1 - c,
        ]
    ).astype(jnp.int32)
    full_cot, y_own, *parts = gather_cot(where, near, cores_swap(near), far, cores_swap(far))

    owners = owner[:, :, 0]
    frame_rows, filled = frame_slots(picked, owners, d, groups)
    row_ids = jnp.arange(rows, dtype=jnp.int32)
    select = ((frame_rows[:, None] == row_ids[None, :]) & (filled[:, None] > 0)).astype(BF16)

    theirs, mine, sel_theirs, sel_mine = down_blocks(core, hidden_act, w_down, select, bw)
    from_core = cores_swap(theirs)
    both = add(mine, from_core).astype(BF16)
    first = jnp.where(low, 2, 0)
    outer = lax.dynamic_slice_in_dim(both, first, 2, 0)
    outer = add(outer, chips_move(outer, INWARD)).astype(BF16)
    inner = chips_move(outer, MIDDLE)
    r_near = at(inner, jnp.where(low, 1, 0))
    r_far = at(inner, jnp.where(low, 0, 1))
    r_pair_sum = chips_move(add(at(both, z ^ 1), r_far).astype(BF16), PAIR)
    y_out = add(x_in, at(both, z), r_pair_sum, r_near).astype(BF16)

    sel = add(sel_mine, cores_swap(sel_theirs)).astype(BF16)
    sel = sel.reshape(2, 2, *sel.shape[1:])
    sel = add(at(sel, z // 2), chips_move(at(sel, 1 - z // 2), FAR)).astype(BF16)
    sel = add(at(sel, z % 2), chips_move(at(sel, 1 - z % 2), PAIR))
    x_sel = jnp.dot(select, x_in, preferred_element_type=F32)
    y_sel = (sel + x_sel).astype(BF16).reshape(2, 2, CAP, bw)
    oy, ox = d // 2, d % 2
    keep_x = lax.dynamic_index_in_dim(y_sel, ox, 1, keepdims=False)
    send_x = lax.dynamic_index_in_dim(y_sel, 1 - ox, 1, keepdims=False)
    held = jnp.stack([keep_x, windows_swap(send_x, 1)])
    keep_y = lax.dynamic_index_in_dim(held, oy, 1, keepdims=False)
    send_y = lax.dynamic_index_in_dim(held, 1 - oy, 1, keepdims=False)
    arrived = jnp.concatenate([keep_y, windows_swap(send_y, 2)])
    arrived = jnp.take(arrived, jnp.arange(groups, dtype=jnp.int32) ^ d, axis=0)
    z_rows = jnp.dot(arrived.reshape(groups * CAP, bw), w_proj, preferred_element_type=F32)
    z_rows = z_rows + cores_swap(z_rows.astype(BF16)).astype(F32)
    z_rows = z_rows + chips_move(z_rows.astype(BF16), PAIR).astype(F32)
    z_rows = z_rows + chips_move(z_rows.astype(BF16), FAR).astype(F32)
    keep = jnp.repeat(occupied_slots(owners, d), pos_embed.shape[0])[:, None]
    dec_hidden = decoder(z_rows, keep, pos_embed, norm_gain[None, :], w_gate_dec, w_up_dec)

    grad_hidden = rows_grad(full_cot, w_down)

    got = [windows_swap(part, flip) for flip, part in enumerate(parts, 1)]
    other = cores_swap(jnp.stack(got))
    scale = 1.0 / groups
    grad_down = weight_grad(core, [(hidden_act, y_own, None)], scale)
    grad_down = weight_grad(
        core,
        [
            (h_x, got[0], 0),
            (h_x, other[0], 1),
            (h_y, got[1], 0),
            (h_y, other[1], 1),
            (h_d0, got[2], None),
            (h_d1, other[2], None),
        ],
        scale,
        grad_down,
    )
    return (y_out, grad_hidden, grad_down, dec_hidden)


def solution(mesh):
    small = dict(mesh.shape) == {"dp": 4, "mp": 8}
    return jax.shard_map(
        small_slice if small else any_mesh,
        mesh=mesh,
        in_specs=(
            P("dp", "mp"),
            P("dp", "mp"),
            P("mp", None),
            P("dp", "mp"),
            P(),
            P(),
            P("mp", None),
            P(),
            P(),
            P(None, "mp"),
            P(None, "mp"),
        ),
        out_specs=(P("dp", "mp"), P("dp", "mp"), P("mp", "dp"), P("dp", "mp")),
        check_vma=False,
    )
```
